32 devices in a mesh: blocks: 32 (over z, y, x, core).
Axes of the slice: x: 2, y: 2, z: 4, core: 2. Of those that a mesh axis runs over, the one named last changes fastest.
Arguments:
- spectra: float32 [1152, 66, 512], P('blocks'), may hold values from 0.05 to 2
- courant: float32 [1152, 3, 512], P('blocks'), may hold values from 0.05 to 0.3
- kernel: bfloat16 [66, 4356], replicated, may hold values from -0.09375 to 0.09375
- old_count: int32 [32], replicated, may hold values from 12 to 36, as said below
- new_count: int32 [32], replicated, may hold values from 12 to 36, as said below
- upwind: int32 [768, 3], replicated, may hold values from 0 to 767, as said below
Outputs:
- updated: float32 [1152, 66, 512], P('blocks')
The draws below stay inside these ranges and needn't reach their ends.
Inputs may be any that keep to these rules, and one draw needn't show every extreme that they name: `old_count`: each count lies in the stated range and both ends are reached in the old and in the new layout; the counts sum to 768; between the two layouts every device boundary along the curve moves by at most 12 blocks, and in every draw some boundary moves by exactly 12 blocks toward higher devices and another by exactly 12 toward lower devices. `new_count`: as old_count, for the new layout. Blocks form aligned runs of 12 along the curve, each run one cross-section of the grid; upwind[b, 0] = b - s * 12 cyclically over 768, where s is +1 or -1 and depends only on b's position within its run, both signs occurring; upwind[b, 1] and upwind[b, 2] lie in the same run as b, arranged alike in every run; every block is upwind of exactly one block per direction.
All inputs are finite; a program needn't handle non-finite values.
Results may differ from the reference program's by a relative error of at most 0.0022.
Values sent between devices are 32-bit elements; how exact they have to be, the bound alone decides.
A program may use at most 128 MiB of HBM per device.

```python
import math
import jax
import jax.numpy as jnp
from jax import lax

BLK_DEV = 24
HALF = 12
CAP = 36
NB = 768
SLOTS = 1152
BINS = 66
EDGE = 8
CELLS = 512
PAIRS = 4356
N_BLOCKS = 32


def boundary_offsets(key):
    base = jax.random.fold_in(key, 4099)
    key_mag, key_sign, key_spot, key_pos = jax.random.split(base, 4)
    device_ids = jnp.arange(N_BLOCKS, dtype=jnp.int32)
    magnitude = jax.random.randint(key_mag, (N_BLOCKS,), HALF // 2, HALF + 1)
    spread_draw = jax.random.randint(key_pos, (N_BLOCKS,), 0, HALF + 1)
    higher = magnitude + spread_draw % (HALF - magnitude + 1)
    lower = higher - magnitude
    upward = jax.random.randint(key_sign, (N_BLOCKS,), 0, 2) == 1
    older = jnp.where(upward, higher, lower)
    newer = jnp.where(upward, lower, higher)
    chosen = jax.random.randint(key_spot, (), 1, N_BLOCKS - 2)
    older = jnp.where(device_ids == 0, 0, older)
    newer = jnp.where(device_ids == 0, 0, newer)
    older = jnp.where(device_ids == chosen - 1, 0, older)
    older = jnp.where(device_ids == chosen, HALF, older)
    older = jnp.where(device_ids == chosen + 1, 0, older)
    newer = jnp.where(device_ids == chosen, 0, newer)
    newer = jnp.where(device_ids == chosen + 1, HALF, newer)
    newer = jnp.where(device_ids == chosen + 2, 0, newer)
    return (older, newer)


def counts_from(offsets):
    return (BLK_DEV + offsets - jnp.roll(offsets, -1)).astype(jnp.int32)


def draw_old_count(key, part):
    return counts_from(boundary_offsets(key)[0])


def draw_new_count(key, part):
    return counts_from(boundary_offsets(key)[1])


def draw_upwind(key, part):
    order = jax.random.permutation(jax.random.fold_in(key, 811), HALF).astype(jnp.int32)
    inverse = jnp.argsort(order).astype(jnp.int32)
    signs = jax.random.randint(jax.random.fold_in(key, 907), (HALF,), 0, 2).astype(jnp.int32) * 2 - 1
    signs = signs.at[order[0]].set(1)
    signs = signs.at[order[1]].set(-1)
    blocks = N_BLOCKS * BLK_DEV
    sections = blocks // HALF
    block_ids = jnp.arange(blocks, dtype=jnp.int32)
    section = block_ids // HALF
    position = block_ids % HALF
    cross = inverse[position]
    across = cross // 2
    depth = cross % 2
    rows_across = HALF // 2
    x_up = (section - signs[position]) % sections * HALF + position
    y_up = section * HALF + order[(across - 1) % rows_across * 2 + depth]
    z_up = section * HALF + order[across * 2 + (1 - depth)]
    return jnp.stack([x_up, y_up, z_up], axis=1).astype(jnp.int32)


def levels(key, dims, cuts, least, high):
    factor_of = 1.0
    for dim, shards_of in cuts:
        draws = jax.random.uniform(jax.random.fold_in(jax.random.fold_in(key, 6), dim), (shards_of,), jnp.float32, least / len(cuts), high / len(cuts))
        factor_of = factor_of * jnp.repeat(jnp.exp(draws), dims[dim] // shards_of).reshape((-1,) + (1,) * (len(dims) - 1 - dim))
    return factor_of


def normal_values(stream_key, extent, scale, most, held_as=jnp.bfloat16):
    entries = scale * jax.random.normal(stream_key, extent, jnp.float32)
    return jnp.clip(entries, min=-most, max=most).astype(held_as)


def setup_inputs(seed: int = 0) -> dict:
    keys = jax.random.split(jax.random.key(seed), 7)
    return {
        "spectra": jnp.clip(jnp.exp(math.log(2.0) - 3.6888794 * jax.random.uniform(keys[0], (SLOTS, BINS, CELLS), jnp.float32) ** levels(keys[0], (SLOTS, BINS, CELLS), ((0, 32),), -0.2, 0.2)), 0.05, 2.0),
        "courant": jnp.clip(0.05 + 0.25 * jax.random.uniform(keys[1], (SLOTS, 3, CELLS), jnp.float32) ** levels(keys[1], (SLOTS, 3, CELLS), ((0, 32),), -0.2, 0.2), 0.05, 0.3),
        "kernel": normal_values(keys[2], (BINS, PAIRS), PAIRS ** -0.5, 0.09375),
        "old_count": draw_old_count(jax.random.fold_in(keys[6], 71), 0),
        "new_count": draw_new_count(jax.random.fold_in(keys[6], 71), 0),
        "upwind": draw_upwind(jax.random.fold_in(keys[6], 71), 0),
    }


def exclusive(counts):
    return jnp.cumsum(counts) - counts


def minmod_value(lower, outer):
    return 0.5 * (jnp.sign(lower) + jnp.sign(outer)) * jnp.minimum(jnp.abs(lower), jnp.abs(outer))


def limited(outer, speeds, upwind_value):
    return speeds * (outer + 0.5 * (1.0 - speeds) * minmod_value(outer - upwind_value, outer))


def slots_of(counts):
    starts = exclusive(counts)
    block_ids = jnp.arange(NB, dtype=jnp.int32)
    owner_ids = jnp.sum((block_ids[:, None] >= starts[None, :]).astype(jnp.int32), axis=1) - 1
    return (owner_ids * CAP + block_ids - starts[owner_ids]).astype(jnp.int32)


def reference(spectra, courant, kernel, old_count, new_count, upwind):
    old_slot = slots_of(old_count)
    state = spectra[old_slot].reshape(NB, BINS, EDGE, EDGE, EDGE)
    speeds = courant[old_slot].reshape(NB, 3, EDGE, EDGE, EDGE)
    fluxes = [speeds[:, direction][:, None] * state for direction in range(3)]
    first = state
    for direction in range(3):
        cell_axis = 2 + direction
        face_in = lax.index_in_dim(fluxes[direction], EDGE - 1, cell_axis, keepdims=True)[upwind[:, direction]]
        inflow = jnp.concatenate([face_in, lax.slice_in_dim(fluxes[direction], 0, EDGE - 1, axis=cell_axis)], axis=cell_axis)
        first = first - fluxes[direction] + inflow
    second = first
    for direction in range(3):
        cell_axis = 2 + direction
        layer_in = lax.index_in_dim(first, EDGE - 1, cell_axis, keepdims=True)[upwind[:, direction]]
        upwind_value = jnp.concatenate([layer_in, lax.slice_in_dim(first, 0, EDGE - 1, axis=cell_axis)], axis=cell_axis)
        cell_flux = limited(first, speeds[:, direction][:, None], upwind_value)
        face_in = lax.index_in_dim(cell_flux, EDGE - 1, cell_axis, keepdims=True)[upwind[:, direction]]
        inflow = jnp.concatenate([face_in, lax.slice_in_dim(cell_flux, 0, EDGE - 1, axis=cell_axis)], axis=cell_axis)
        second = second - cell_flux + inflow
    grouped = second.reshape(NB, BINS, CELLS)

    def coalesce(block):
        pair_terms = (block[:, None, :] * block[None, :, :]).reshape(PAIRS, CELLS).astype(jnp.bfloat16)
        return block + jnp.dot(kernel, pair_terms, preferred_element_type=jnp.float32)

    coalesced = lax.map(coalesce, grouped)
    new_slot = slots_of(new_count)
    return jnp.zeros((SLOTS, BINS, CELLS), jnp.float32).at[new_slot].set(coalesced)
```

```python
import functools

import jax
import jax.numpy as jnp
from jax import lax
from jax.experimental import pallas as pl
from jax.experimental.pallas import tpu as pltpu
from jax.sharding import PartitionSpec as P

HALF = 12
BINS = 66
EDGE = 8
CELLS = 512
YZ = 6
PACK = HALF * 64 + 2 * CELLS
ROWS = 72
STRIDES = (64, 8, 1)
KDIM = 2816
VMEM_LIMIT = 63 * 1024 * 1024
CHUNKS = ((0, 16), (16, 32), (32, 48), (48, 64), (64, 66))
F32 = jnp.float32

T_OC, T_NC, T_OS, T_NS = 0, 1, 2, 3
T_SEND = 8
T_SRC = 32


def lane_coord(direction, rows):
    lane = lax.broadcasted_iota(jnp.int32, (rows, CELLS), 1)
    return (lane // STRIDES[direction]) % EDGE


def table_kernel(n, capacity, meta, tab):
    me = meta[0]

    def total(base, count):
        return lax.fori_loop(0, count, lambda i, s: s + meta[base + i], jnp.int32(0))

    old_start, new_start = total(1, me), total(1 + n, me)
    oc, nc = meta[1 + me], meta[1 + n + me]
    tab[T_OC] = oc
    tab[T_NC] = nc
    tab[T_OS] = old_start
    tab[T_NS] = new_start
    base = 1 + 2 * n
    end = old_start + oc
    zero = jnp.int32(0)
    end_run = lax.rem(end, HALF)
    start_run = lax.rem(old_start, HALF)

    def up(t, d):
        return meta[base + 3 * t + d] - HALF

    for d in (1, 2):
        for k in range(YZ):
            tab[T_SEND + (d - 1) * YZ + k] = zero
            tab[T_SEND + 2 * YZ + (d - 1) * YZ + k] = zero

    def block_src(b, carry):
        pos = lax.rem(old_start + b, HALF)
        rel = meta[base + 3 * pos] - HALF - pos
        u = b + rel
        tab[T_SRC + 3 * b] = jnp.where(
            u < 0, capacity + HALF + u, jnp.where(u >= oc, capacity + HALF + u - oc, u)
        )
        for d in (1, 2):
            tab[T_SRC + 3 * b + d] = jnp.clip(b + up(pos, d) - pos, 0, capacity - 1)
        return carry

    lax.fori_loop(0, capacity, block_src, zero)

    for d in (1, 2):
        pool = capacity + 2 * HALF + (d - 1) * 2 * YZ

        def link(t, counts):
            s_up, s_dn, r_up, r_dn = counts
            u = up(t, d)
            cross = (t >= end_run) & (u < end_run)

            @pl.when(cross)
            def _():
                tab[T_SEND + (d - 1) * YZ + s_up] = jnp.clip(oc - end_run + u, 0, capacity - 1)

            s_up = s_up + cross.astype(jnp.int32)
            cross = (t < end_run) & (u >= end_run)
            b = oc - end_run + t

            @pl.when(cross & (b >= 0))
            def _():
                tab[T_SRC + 3 * b + d] = pool + YZ + r_dn

            r_dn = r_dn + cross.astype(jnp.int32)
            cross = (t < start_run) & (u >= start_run)

            @pl.when(cross)
            def _():
                tab[T_SEND + 2 * YZ + (d - 1) * YZ + s_dn] = jnp.clip(
                    u - start_run, 0, capacity - 1
                )

            s_dn = s_dn + cross.astype(jnp.int32)
            cross = (t >= start_run) & (u < start_run)

            @pl.when(cross)
            def _():
                tab[T_SRC + 3 * jnp.minimum(t - start_run, capacity - 1) + d] = pool + r_up

            r_up = r_up + cross.astype(jnp.int32)
            return s_up, s_dn, r_up, r_dn

        lax.fori_loop(0, HALF, link, (zero, zero, zero, zero))


def pack(out, field, tab):
    oc = tab[T_OC]
    for r0, r1 in CHUNKS:
        low = lax.broadcasted_iota(jnp.int32, (r1 - r0, 128), 1) < 64
        coords = [lane_coord(d, r1 - r0) for d in (1, 2)]
        for side in range(2):
            first = oc - HALF if side == 0 else 0
            for j in range(0, HALF, 2):
                a = field(first + j, 0, r0, r1)[:, 384:]
                b = field(first + j + 1, 0, r0, r1)[:, 384:]
                out(side, r0, r1, 64 * j, jnp.where(low, pltpu.roll(a, 64, 1), b))
            for d in (1, 2):
                total = jnp.zeros((r1 - r0, CELLS), F32)
                for k in range(YZ):
                    block = tab[T_SEND + side * 2 * YZ + (d - 1) * YZ + k]
                    value = field(block, d, r0, r1)
                    shift = (CELLS - STRIDES[d] * (EDGE - 1 - k)) % CELLS
                    total = jnp.where(coords[d - 1] == k, pltpu.roll(value, shift, 1), total)
                out(side, r0, r1, HALF * 64 + (d - 1) * CELLS, total)


def unpack(packet, place, capacity):
    for r0, r1 in CHUNKS:
        for side in range(2):
            for j in range(HALF):
                value = packet(side, r0, r1, 128 * (j // 2), 128)
                if j % 2 == 0:
                    value = pltpu.roll(value, 64, 1)
                place(capacity + side * HALF + j, r0, r1, 384, value, 0)
            for d in (1, 2):
                value = packet(side, r0, r1, HALF * 64 + (d - 1) * CELLS, CELLS)
                for k in range(YZ):
                    slot = capacity + 2 * HALF + (d - 1) * 2 * YZ + side * YZ + k
                    place(slot, r0, r1, 0, pltpu.roll(value, STRIDES[d] * (EDGE - 1 - k), 1), d)


def shifted(value, upwind, direction, coord):
    if direction:
        upwind = pltpu.roll(upwind, CELLS - STRIDES[direction - 1], 1)
    return pltpu.roll(jnp.where(coord == EDGE - 1, upwind, value), STRIDES[direction], 1)


def faces_kernel(n, capacity, meta, q0, cs, tab, up, dn):
    table_kernel(n, capacity, meta, tab)
    outs = (up, dn)

    def field(block, d, r0, r1):
        return q0[block, r0:r1, :] * cs[block, d : d + 1, :]

    def out(side, r0, r1, lane, value):
        outs[side][r0:r1, lane : lane + value.shape[1]] = value

    pack(out, field, tab)


def first_kernel(capacity, tab, q0, cs, from_prev, from_next, q1, up, dn, pool):
    packets = (from_prev, from_next)

    def place(slot, r0, r1, l0, value, d):
        pool[slot - capacity, r0:r1, l0 : l0 + value.shape[1]] = value

    unpack(
        lambda side, r0, r1, lane, width: packets[side][r0:r1, lane : lane + width],
        place,
        capacity,
    )

    def step(b, carry):
        srcs = [tab[T_SRC + 3 * b + d] for d in range(3)]
        local = [jnp.minimum(s, capacity - 1) for s in srcs]
        far = [jnp.maximum(s - capacity, 0) for s in srcs]
        remote = [s >= capacity for s in srcs]
        for r0, r1 in CHUNKS:
            q = q0[b, r0:r1, :]
            result = q
            for d in range(3):
                coord = lane_coord(d, r1 - r0)
                flux = q * cs[b, d : d + 1, :]
                near = q0[local[d], r0:r1, :] * cs[local[d], d : d + 1, :]
                upwind = jnp.where(remote[d], pool[far[d], r0:r1, :], near)
                result = result - flux + shifted(flux, upwind, d, coord)
            q1[b, r0:r1, :] = result
        return carry

    lax.fori_loop(0, tab[T_OC], step, 0)

    outs = (up, dn)

    def flux_field(block, d, r0, r1):
        q = q1[block, r0:r1, :]
        c = cs[block, d : d + 1, :]
        m = q - pltpu.roll(q, STRIDES[d], 1)
        m = jnp.maximum(jnp.minimum(m, q), 0.0)
        return c * (q + (0.5 * (1.0 - c)) * m)

    def layer_field(block, d, r0, r1):
        return q1[block, r0:r1, :]

    for part, field in enumerate((flux_field, layer_field)):

        def out(side, r0, r1, lane, value, part=part):
            outs[side][part, r0:r1, lane : lane + value.shape[1]] = value

        pack(out, field, tab)


def second_kernel(
    capacity, tab, q1, cs, from_prev, from_next, q2, mig_up, mig_dn, lpool, fx, fy, fz
):
    packets = (from_prev, from_next)
    fluxes = (fx, fy, fz)
    bases = (capacity, capacity + 2 * HALF, capacity + 2 * HALF + 2 * YZ)

    def place_layer(slot, r0, r1, l0, value, d):
        lpool[slot - capacity, r0:r1, l0 : l0 + value.shape[1]] = value

    def place_flux(slot, r0, r1, l0, value, d):
        fluxes[d][slot - bases[d] + capacity, r0:r1, l0 : l0 + value.shape[1]] = value

    for part, place in enumerate((place_flux, place_layer)):
        unpack(
            lambda side, r0, r1, lane, width, part=part: packets[side][
                part, r0:r1, lane : lane + width
            ],
            place,
            capacity,
        )

    def limit(b, carry):
        for d in range(3):
            src = tab[T_SRC + 3 * b + d]
            local = jnp.minimum(src, capacity - 1)
            far = jnp.maximum(src - capacity, 0)
            remote = src >= capacity
            c = cs[b, d : d + 1, :]
            half = 0.5 * (1.0 - c)
            for r0, r1 in CHUNKS:
                coord = lane_coord(d, r1 - r0)
                q = q1[b, r0:r1, :]
                upwind = jnp.where(remote, lpool[far, r0:r1, :], q1[local, r0:r1, :])
                m = q - shifted(q, upwind, d, coord)
                m = jnp.maximum(jnp.minimum(m, q), 0.0)
                fluxes[d][b, r0:r1, :] = c * (q + half * m)
        return carry

    lax.fori_loop(0, tab[T_OC], limit, 0)

    def step(b, carry):
        srcs = [tab[T_SRC + 3 * b + d] for d in range(3)]
        srcs = [
            jnp.where(srcs[d] >= capacity, srcs[d] - bases[d] + capacity, srcs[d])
            for d in range(3)
        ]
        for r0, r1 in CHUNKS:
            result = q1[b, r0:r1, :]
            for d in range(3):
                coord = lane_coord(d, r1 - r0)
                flux = fluxes[d][b, r0:r1, :]
                upwind = fluxes[d][srcs[d], r0:r1, :]
                result = result - flux + shifted(flux, upwind, d, coord)
            q2[b, r0:r1, :] = result
        return carry

    oc = tab[T_OC]
    lax.fori_loop(0, oc, step, 0)

    def copy(j, carry):
        mig_up[j] = q2[oc - HALF + j]
        mig_dn[j] = q2[j]
        return carry

    lax.fori_loop(0, HALF, copy, 0)


def build_pairs(q, qp, pairs):
    qp[0:BINS, :] = q
    qp[BINS : BINS + 1, :] = q[BINS - 1 : BINS, :]
    qp[BINS + 1 : BINS + 2, :] = q[BINS - 2 : BINS - 1, :]
    qp[BINS + 2 : ROWS, :] = jnp.zeros((ROWS - BINS - 2, CELLS), F32)
    row = lax.broadcasted_iota(jnp.int32, (8, CELLS), 0)
    pending = None
    at = 0
    for i in range(BINS - 2):
        lead = jnp.broadcast_to(qp[i : i + 1, :], (8, CELLS))
        for g in range(i // 8, ROWS // 8):
            by = lead
            if i < 2 and g == ROWS // 8 - 1:
                by = jnp.where(row < 2, lead, qp[BINS - 1 - i : BINS - i, :])
            term = by * qp[8 * g : 8 * g + 8, :]
            if pending is None:
                pending = term
            else:
                tile = jnp.concatenate([pending, term], axis=0)
                pairs[at : at + 16, :] = tile.astype(jnp.bfloat16)
                pending = None
                at += 16


def coalesce_range(lo, hi, load, w, out, qps, pairs, res, sems):
    def copy_out(slot, buf):
        return pltpu.make_async_copy(res.at[buf], out.at[slot], sems.at[buf])

    count = hi - lo

    def body(it, carry):
        first = lo + 2 * it
        slots = (first, jnp.minimum(first + 1, hi - 1))
        values = [load(s) for s in slots]

        @pl.when(it > 0)
        def _():
            for buf in range(2):
                copy_out(lo, buf).wait()

        for buf in range(2):
            build_pairs(values[buf], qps[buf], pairs[buf])
        for buf in range(2):
            gain = jnp.dot(w[...], pairs[buf][...], preferred_element_type=F32)
            res[buf] = qps[buf][0:BINS, :] + gain
        copy_out(slots[0], 0).start()

        @pl.when(first + 1 < hi)
        def _():
            copy_out(slots[1], 1).start()

        return carry

    trips = lax.div(count + 1, 2)
    lax.fori_loop(0, trips, body, 0)

    @pl.when(trips > 0)
    def _():
        copy_out(lo, 0).wait()

    @pl.when((trips > 0) & (lax.rem(count, 2) == 0))
    def _():
        copy_out(lo, 1).wait()


def stay_kernel(capacity, tab, q2, w, out, qpa, qpb, pa, pb, res, zero, sems, zsem):
    oc, nc, old, new = tab[T_OC], tab[T_NC], tab[T_OS], tab[T_NS]
    zero[...] = jnp.zeros_like(zero)

    def blank(slot):
        return pltpu.make_async_copy(zero, out.at[slot], zsem)

    def start(slot, carry):
        blank(slot).start()
        return carry

    def wait(slot, carry):
        blank(slot).wait()
        return carry

    lax.fori_loop(nc, capacity, start, 0)
    lo = jnp.clip(old - new, 0, nc)
    hi = jnp.clip(old + oc - new, lo, nc)
    coalesce_range(
        lo, hi, lambda s: q2[s + new - old], w, out, (qpa, qpb), (pa, pb), res, sems
    )
    lax.fori_loop(nc, capacity, wait, 0)


def come_kernel(capacity, tab, from_prev, from_next, w, old_out, out, qpa, qpb, pa, pb, res, sems):
    oc, nc, old, new = tab[T_OC], tab[T_NC], tab[T_OS], tab[T_NS]
    args = (w, out, (qpa, qpb), (pa, pb), res, sems)
    coalesce_range(
        jnp.int32(0),
        jnp.clip(old - new, 0, nc),
        lambda s: from_prev[s + new - old + HALF],
        *args,
    )
    coalesce_range(
        jnp.clip(old + oc - new, 0, nc),
        nc,
        lambda s: from_next[s + new - old - oc],
        *args,
    )


def folded_kernel(kernel):
    cube = kernel.reshape(BINS, BINS, BINS).astype(F32)
    turned = jnp.swapaxes(cube, 1, 2)
    i = lax.broadcasted_iota(jnp.int32, cube.shape, 1)
    j = lax.broadcasted_iota(jnp.int32, cube.shape, 2)
    folded = jnp.where(i < j, cube + turned, jnp.where(i == j, cube, 0.0))
    a, b = BINS - 2, BINS - 1
    extra = jnp.zeros((BINS, BINS, ROWS - BINS), F32)
    extra = extra.at[:, 0, 0].set(cube[:, b, b])
    extra = extra.at[:, 1, 0].set(cube[:, a, b] + cube[:, b, a])
    extra = extra.at[:, 1, 1].set(cube[:, a, a])
    wide = jnp.concatenate([folded, extra], axis=2).astype(jnp.bfloat16)
    parts = [
        wide[:, 8 * c : 8 * c + 8, 8 * c :].reshape(BINS, -1) for c in range(BINS // 8)
    ]
    return jnp.concatenate(parts, axis=1)


def on_device(n, spectra, courant, kernel, old_count, new_count, upwind):
    capacity = spectra.shape[0]
    shape = jax.ShapeDtypeStruct
    vmem = pl.BlockSpec(memory_space=pltpu.VMEM)
    smem = pl.BlockSpec(memory_space=pltpu.SMEM)
    hbm = pl.BlockSpec(memory_space=pl.ANY)
    params = pltpu.CompilerParams(vmem_limit_bytes=VMEM_LIMIT)
    blocks = shape((capacity, BINS, CELLS), F32)
    half = shape((HALF, BINS, CELLS), F32)

    def cost(flops, nbytes):
        return pl.CostEstimate(flops=flops, bytes_accessed=nbytes, transcendentals=0)

    meta = jnp.concatenate(
        [
            lax.axis_index("blocks").astype(jnp.int32)[None],
            old_count,
            new_count,
            upwind[HALF : 2 * HALF].reshape(-1),
        ]
    )
    tab, up, dn = pl.pallas_call(
        functools.partial(faces_kernel, n, capacity),
        out_shape=(
            shape((T_SRC + 3 * capacity,), jnp.int32),
            shape((BINS, PACK), F32),
            shape((BINS, PACK), F32),
        ),
        in_specs=[smem, vmem, vmem],
        out_specs=(smem, vmem, vmem),
        compiler_params=params,
        name="faces",
    )(meta, spectra, courant)

    def along(value, step, ring):
        route = [(i, i + step) for i in range(n)]
        if ring:
            route = [(i, j % n) for i, j in route]
        return lax.ppermute(value, "blocks", [(i, j) for i, j in route if 0 <= j < n])

    from_prev, from_next = along(up, 1, True), along(dn, -1, True)
    weights = folded_kernel(kernel)
    q1, up, dn = pl.pallas_call(
        functools.partial(first_kernel, capacity),
        out_shape=(blocks, shape((2, BINS, PACK), F32), shape((2, BINS, PACK), F32)),
        in_specs=[smem, vmem, vmem, vmem, vmem],
        out_specs=(vmem, vmem, vmem),
        scratch_shapes=[pltpu.VMEM((2 * HALF + 4 * YZ, BINS, CELLS), F32)],
        compiler_params=params,
        name="first",
    )(tab, spectra, courant, from_prev, from_next)
    from_prev, from_next = along(up, 1, True), along(dn, -1, True)
    q2, up, dn = pl.pallas_call(
        functools.partial(second_kernel, capacity),
        out_shape=(blocks, half, half),
        in_specs=[smem, vmem, vmem, vmem, vmem],
        out_specs=(vmem, vmem, vmem),
        scratch_shapes=[
            pltpu.VMEM((2 * HALF + 4 * YZ, BINS, CELLS), F32),
            pltpu.VMEM((capacity + 2 * HALF, BINS, CELLS), F32),
            pltpu.VMEM((capacity + 2 * YZ, BINS, CELLS), F32),
            pltpu.VMEM((capacity + 2 * YZ, BINS, CELLS), F32),
        ],
        compiler_params=params,
        name="second",
    )(tab, q1, courant, from_prev, from_next)
    from_prev, from_next = along(up, 1, False), along(dn, -1, False)
    buffers = [
        pltpu.VMEM((ROWS, CELLS), F32),
        pltpu.VMEM((ROWS, CELLS), F32),
        pltpu.VMEM((KDIM, CELLS), jnp.bfloat16),
        pltpu.VMEM((KDIM, CELLS), jnp.bfloat16),
        pltpu.VMEM((2, BINS, CELLS), F32),
    ]
    work = 2 * BINS * KDIM * CELLS
    updated = pl.pallas_call(
        functools.partial(stay_kernel, capacity),
        out_shape=blocks,
        in_specs=[smem, vmem, vmem],
        out_specs=hbm,
        scratch_shapes=buffers
        + [
            pltpu.VMEM((BINS, CELLS), F32),
            pltpu.SemaphoreType.DMA((2,)),
            pltpu.SemaphoreType.DMA,
        ],
        compiler_params=params,
        cost_estimate=cost(24 * work, 12 * 1024 * 1024),
        name="stay",
    )(tab, q2, weights)
    return pl.pallas_call(
        functools.partial(come_kernel, capacity),
        out_shape=blocks,
        in_specs=[smem, vmem, vmem, vmem, hbm],
        out_specs=hbm,
        input_output_aliases={4: 0},
        scratch_shapes=buffers + [pltpu.SemaphoreType.DMA((2,))],
        compiler_params=params,
        cost_estimate=cost(12 * work, 6 * 1024 * 1024),
        name="come",
    )(tab, from_prev, from_next, weights, updated)


def solution(mesh):
    in_specs = (P("blocks", None, None), P("blocks", None, None), P(), P(), P(), P())
    out_specs = P("blocks", None, None)
    return jax.shard_map(
        functools.partial(on_device, mesh.shape["blocks"]),
        mesh=mesh,
        in_specs=in_specs,
        out_specs=out_specs,
        check_vma=False,
    )
```

```python
import functools

import jax
import jax.numpy as jnp
from jax import lax
from jax.experimental import pallas as pl
from jax.experimental.pallas import tpu as pltpu
from jax.sharding import PartitionSpec as P

HALF = 12
BINS = 66
EDGE = 8
CELLS = 512
YZ = 6
PACK = HALF * 64 + 2 * CELLS
ROWS = 72
STRIDES = (64, 8, 1)
KDIM = 2816
VMEM_LIMIT = 63 * 1024 * 1024
CHUNKS = ((0, 16), (16, 32), (32, 48), (48, 64), (64, 66))
F32 = jnp.float32

T_OC, T_NC, T_OS, T_NS = 0, 1, 2, 3
T_SEND = 8
T_SRC = 32


def lane_coord(direction, rows):
    lane = lax.broadcasted_iota(jnp.int32, (rows, CELLS), 1)
    return (lane // STRIDES[direction]) % EDGE


def table_kernel(n, capacity, meta, tab):
    me = meta[0]

    def total(base, count):
        return lax.fori_loop(0, count, lambda i, s: s + meta[base + i], jnp.int32(0))

    old_start, new_start = total(1, me), total(1 + n, me)
    oc, nc = meta[1 + me], meta[1 + n + me]
    tab[T_OC] = oc
    tab[T_NC] = nc
    tab[T_OS] = old_start
    tab[T_NS] = new_start
    base = 1 + 2 * n
    end = old_start + oc
    zero = jnp.int32(0)
    end_run = lax.rem(end, HALF)
    start_run = lax.rem(old_start, HALF)

    def up(t, d):
        return meta[base + 3 * t + d] - HALF

    for d in (1, 2):
        for k in range(YZ):
            tab[T_SEND + (d - 1) * YZ + k] = zero
            tab[T_SEND + 2 * YZ + (d - 1) * YZ + k] = zero

    def block_src(b, carry):
        pos = lax.rem(old_start + b, HALF)
        rel = meta[base + 3 * pos] - HALF - pos
        u = b + rel
        tab[T_SRC + 3 * b] = jnp.where(
            u < 0, capacity + HALF + u, jnp.where(u >= oc, capacity + HALF + u - oc, u)
        )
        for d in (1, 2):
            tab[T_SRC + 3 * b + d] = jnp.clip(b + up(pos, d) - pos, 0, capacity - 1)
        return carry

    lax.fori_loop(0, capacity, block_src, zero)

    for d in (1, 2):
        pool = capacity + 2 * HALF + (d - 1) * 2 * YZ

        def link(t, counts):
            s_up, s_dn, r_up, r_dn = counts
            u = up(t, d)
            cross = (t >= end_run) & (u < end_run)

            @pl.when(cross)
            def _():
                tab[T_SEND + (d - 1) * YZ + s_up] = jnp.clip(oc - end_run + u, 0, capacity - 1)

            s_up = s_up + cross.astype(jnp.int32)
            cross = (t < end_run) & (u >= end_run)
            b = oc - end_run + t

            @pl.when(cross & (b >= 0))
            def _():
                tab[T_SRC + 3 * b + d] = pool + YZ + r_dn

            r_dn = r_dn + cross.astype(jnp.int32)
            cross = (t < start_run) & (u >= start_run)

            @pl.when(cross)
            def _():
                tab[T_SEND + 2 * YZ + (d - 1) * YZ + s_dn] = jnp.clip(
                    u - start_run, 0, capacity - 1
                )

            s_dn = s_dn + cross.astype(jnp.int32)
            cross = (t >= start_run) & (u < start_run)

            @pl.when(cross)
            def _():
                tab[T_SRC + 3 * jnp.minimum(t - start_run, capacity - 1) + d] = pool + r_up

            r_up = r_up + cross.astype(jnp.int32)
            return s_up, s_dn, r_up, r_dn

        lax.fori_loop(0, HALF, link, (zero, zero, zero, zero))


def pack(out, field, tab):
    oc = tab[T_OC]
    for r0, r1 in CHUNKS:
        low = lax.broadcasted_iota(jnp.int32, (r1 - r0, 128), 1) < 64
        coords = [lane_coord(d, r1 - r0) for d in (1, 2)]
        for side in range(2):
            first = oc - HALF if side == 0 else 0
            for j in range(0, HALF, 2):
                a = field(first + j, 0, r0, r1)[:, 384:]
                b = field(first + j + 1, 0, r0, r1)[:, 384:]
                out(side, r0, r1, 64 * j, jnp.where(low, pltpu.roll(a, 64, 1), b))
            for d in (1, 2):
                total = jnp.zeros((r1 - r0, CELLS), F32)
                for k in range(YZ):
                    block = tab[T_SEND + side * 2 * YZ + (d - 1) * YZ + k]
                    value = field(block, d, r0, r1)
                    shift = (CELLS - STRIDES[d] * (EDGE - 1 - k)) % CELLS
                    total = jnp.where(coords[d - 1] == k, pltpu.roll(value, shift, 1), total)
                out(side, r0, r1, HALF * 64 + (d - 1) * CELLS, total)


def unpack(packet, place, capacity):
    for r0, r1 in CHUNKS:
        for side in range(2):
            for j in range(HALF):
                value = packet(side, r0, r1, 128 * (j // 2), 128)
                if j % 2 == 0:
                    value = pltpu.roll(value, 64, 1)
                place(capacity + side * HALF + j, r0, r1, 384, value, 0)
            for d in (1, 2):
                value = packet(side, r0, r1, HALF * 64 + (d - 1) * CELLS, CELLS)
                for k in range(YZ):
                    slot = capacity + 2 * HALF + (d - 1) * 2 * YZ + side * YZ + k
                    place(slot, r0, r1, 0, pltpu.roll(value, STRIDES[d] * (EDGE - 1 - k), 1), d)


def shifted(value, upwind, direction, coord):
    if direction:
        upwind = pltpu.roll(upwind, CELLS - STRIDES[direction - 1], 1)
    return pltpu.roll(jnp.where(coord == EDGE - 1, upwind, value), STRIDES[direction], 1)


def faces_kernel(n, capacity, meta, q0, cs, tab, up, dn):
    table_kernel(n, capacity, meta, tab)
    outs = (up, dn)

    def field(block, d, r0, r1):
        return q0[block, r0:r1, :] * cs[block, d : d + 1, :]

    def out(side, r0, r1, lane, value):
        outs[side][r0:r1, lane : lane + value.shape[1]] = value

    pack(out, field, tab)


def sources(tab, b, capacity):
    srcs = [tab[T_SRC + 3 * b + d] for d in range(3)]
    near = [jnp.minimum(s, capacity - 1) for s in srcs]
    far = [jnp.maximum(s - capacity, 0) for s in srcs]
    away = [s >= capacity for s in srcs]
    return near, far, away


def first_block(b, where, q0, cs, q1, pool):
    near, far, away = where
    for r0, r1 in CHUNKS:
        q = q0[b, r0:r1, :]
        result = q
        for d in range(3):
            coord = lane_coord(d, r1 - r0)
            flux = q * cs[b, d : d + 1, :]
            upwind = q0[near[d], r0:r1, :] * cs[near[d], d : d + 1, :]
            if pool is not None:
                upwind = jnp.where(away[d], pool[far[d], r0:r1, :], upwind)
            result = result - flux + shifted(flux, upwind, d, coord)
        q1[b, r0:r1, :] = result


def limited(q, before, c):
    m = jnp.maximum(jnp.minimum(q - before, q), 0.0)
    return c * (q + (0.5 * (1.0 - c)) * m)


def second_block(b, where, q1, cs, q2, lpool, fpool):
    near, far, away = where
    for r0, r1 in CHUNKS:
        q = q1[b, r0:r1, :]
        result = q
        for d in range(3):
            coord = lane_coord(d, r1 - r0)
            layer = q1[near[d], r0:r1, :]
            inflow = limited(layer, pltpu.roll(layer, STRIDES[d], 1), cs[near[d], d : d + 1, :])
            if lpool is not None:
                layer = jnp.where(away[d], lpool[far[d], r0:r1, :], layer)
                inflow = jnp.where(away[d], fpool[far[d], r0:r1, :], inflow)
            flux = limited(q, shifted(q, layer, d, coord), cs[b, d : d + 1, :])
            result = result - flux + shifted(flux, inflow, d, coord)
        q2[b, r0:r1, :] = result


def near_kernel(capacity, advance, tab, q, cs, out):
    def step(b, carry):
        where = sources(tab, b, capacity)
        away = where[2]

        @pl.when(jnp.logical_not(away[0] | away[1] | away[2]))
        def _():
            advance(b, where, q, cs, out)

        return carry

    lax.fori_loop(0, tab[T_OC], step, 0)


def far_blocks(capacity, tab, done, out, advance):
    def step(b, carry):
        where = sources(tab, b, capacity)
        any_away = where[2][0] | where[2][1] | where[2][2]

        @pl.when(any_away)
        def _():
            advance(b, where)

        @pl.when(jnp.logical_not(any_away))
        def _():
            out[b] = done[b]

        return carry

    lax.fori_loop(0, tab[T_OC], step, 0)


def placer(pool, capacity):
    def place(slot, r0, r1, l0, value, d):
        pool[slot - capacity, r0:r1, l0 : l0 + value.shape[1]] = value

    return place


def reader(packets, part):
    def read(side, r0, r1, lane, width):
        return packets[side][r0:r1, part * PACK + lane : part * PACK + lane + width]

    return read


def first_kernel(capacity, tab, q0, cs, from_prev, from_next, done, q1, up, dn, pool):
    unpack(reader((from_prev, from_next), 0), placer(pool, capacity), capacity)
    far_blocks(
        capacity, tab, done, q1, lambda b, where: first_block(b, where, q0, cs, q1, pool)
    )
    outs = (up, dn)

    def flux_field(block, d, r0, r1):
        q = q1[block, r0:r1, :]
        return limited(q, pltpu.roll(q, STRIDES[d], 1), cs[block, d : d + 1, :])

    def layer_field(block, d, r0, r1):
        return q1[block, r0:r1, :]

    for part, field in enumerate((flux_field, layer_field)):

        def out(side, r0, r1, lane, value, part=part):
            lane = lane + part * PACK
            outs[side][r0:r1, lane : lane + value.shape[1]] = value

        pack(out, field, tab)


def second_kernel(
    capacity, tab, q1, cs, from_prev, from_next, done, q2, mig_up, mig_dn, lpool, fpool
):
    for part, pool in enumerate((fpool, lpool)):
        unpack(reader((from_prev, from_next), part), placer(pool, capacity), capacity)
    far_blocks(
        capacity,
        tab,
        done,
        q2,
        lambda b, where: second_block(b, where, q1, cs, q2, lpool, fpool),
    )
    oc = tab[T_OC]

    def copy(j, carry):
        mig_up[j] = q2[oc - HALF + j]
        mig_dn[j] = q2[j]
        return carry

    lax.fori_loop(0, HALF, copy, 0)


def build_pairs(q, qp, pairs):
    qp[0:BINS, :] = q
    qp[BINS : BINS + 1, :] = q[BINS - 1 : BINS, :]
    qp[BINS + 1 : BINS + 2, :] = q[BINS - 2 : BINS - 1, :]
    qp[BINS + 2 : ROWS, :] = jnp.zeros((ROWS - BINS - 2, CELLS), F32)
    row = lax.broadcasted_iota(jnp.int32, (8, CELLS), 0)
    pending = None
    at = 0
    for i in range(BINS - 2):
        lead = jnp.broadcast_to(qp[i : i + 1, :], (8, CELLS))
        for g in range(i // 8, ROWS // 8):
            by = lead
            if i < 2 and g == ROWS // 8 - 1:
                by = jnp.where(row < 2, lead, qp[BINS - 1 - i : BINS - i, :])
            term = by * qp[8 * g : 8 * g + 8, :]
            if pending is None:
                pending = term
            else:
                tile = jnp.concatenate([pending, term], axis=0)
                pairs[at : at + 16, :] = tile.astype(jnp.bfloat16)
                pending = None
                at += 16


def coalesce_range(lo, hi, load, w, out, qps, pairs, res, sems):
    def copy_out(slot, buf):
        return pltpu.make_async_copy(res.at[buf], out.at[slot], sems.at[buf])

    count = hi - lo

    def body(it, carry):
        first = lo + 2 * it
        slots = (first, jnp.minimum(first + 1, hi - 1))
        values = [load(s) for s in slots]

        @pl.when(it > 0)
        def _():
            for buf in range(2):
                copy_out(lo, buf).wait()

        for buf in range(2):
            build_pairs(values[buf], qps[buf], pairs[buf])
        for buf in range(2):
            gain = jnp.dot(w[...], pairs[buf][...], preferred_element_type=F32)
            res[buf] = qps[buf][0:BINS, :] + gain
        copy_out(slots[0], 0).start()

        @pl.when(first + 1 < hi)
        def _():
            copy_out(slots[1], 1).start()

        return carry

    trips = lax.div(count + 1, 2)
    lax.fori_loop(0, trips, body, 0)

    @pl.when(trips > 0)
    def _():
        copy_out(lo, 0).wait()

    @pl.when((trips > 0) & (lax.rem(count, 2) == 0))
    def _():
        copy_out(lo, 1).wait()


def stay_kernel(capacity, tab, q2, w, out, qpa, qpb, pa, pb, res, zero, sems, zsem):
    oc, nc, old, new = tab[T_OC], tab[T_NC], tab[T_OS], tab[T_NS]
    zero[...] = jnp.zeros_like(zero)

    def blank(slot):
        return pltpu.make_async_copy(zero, out.at[slot], zsem)

    def start(slot, carry):
        blank(slot).start()
        return carry

    def wait(slot, carry):
        blank(slot).wait()
        return carry

    lax.fori_loop(nc, capacity, start, 0)
    lo = jnp.clip(old - new, 0, nc)
    hi = jnp.clip(old + oc - new, lo, nc)
    coalesce_range(
        lo, hi, lambda s: q2[s + new - old], w, out, (qpa, qpb), (pa, pb), res, sems
    )
    lax.fori_loop(nc, capacity, wait, 0)


def come_kernel(capacity, tab, from_prev, from_next, w, old_out, out, qpa, qpb, pa, pb, res, sems):
    oc, nc, old, new = tab[T_OC], tab[T_NC], tab[T_OS], tab[T_NS]
    args = (w, out, (qpa, qpb), (pa, pb), res, sems)
    coalesce_range(
        jnp.int32(0),
        jnp.clip(old - new, 0, nc),
        lambda s: from_prev[s + new - old + HALF],
        *args,
    )
    coalesce_range(
        jnp.clip(old + oc - new, 0, nc),
        nc,
        lambda s: from_next[s + new - old - oc],
        *args,
    )


def folded_kernel(kernel):
    cube = kernel.reshape(BINS, BINS, BINS).astype(F32)
    turned = jnp.swapaxes(cube, 1, 2)
    i = lax.broadcasted_iota(jnp.int32, cube.shape, 1)
    j = lax.broadcasted_iota(jnp.int32, cube.shape, 2)
    folded = jnp.where(i < j, cube + turned, jnp.where(i == j, cube, 0.0))
    a, b = BINS - 2, BINS - 1
    extra = jnp.zeros((BINS, BINS, ROWS - BINS), F32)
    extra = extra.at[:, 0, 0].set(cube[:, b, b])
    extra = extra.at[:, 1, 0].set(cube[:, a, b] + cube[:, b, a])
    extra = extra.at[:, 1, 1].set(cube[:, a, a])
    wide = jnp.concatenate([folded, extra], axis=2).astype(jnp.bfloat16)
    parts = [
        wide[:, 8 * c : 8 * c + 8, 8 * c :].reshape(BINS, -1) for c in range(BINS // 8)
    ]
    return jnp.concatenate(parts, axis=1)


def on_device(n, spectra, courant, kernel, old_count, new_count, upwind):
    capacity = spectra.shape[0]
    shape = jax.ShapeDtypeStruct
    vmem = pl.BlockSpec(memory_space=pltpu.VMEM)
    smem = pl.BlockSpec(memory_space=pltpu.SMEM)
    hbm = pl.BlockSpec(memory_space=pl.ANY)
    params = pltpu.CompilerParams(vmem_limit_bytes=VMEM_LIMIT)
    blocks = shape((capacity, BINS, CELLS), F32)
    half = shape((HALF, BINS, CELLS), F32)

    def cost(flops, nbytes):
        return pl.CostEstimate(flops=flops, bytes_accessed=nbytes, transcendentals=0)

    meta = jnp.concatenate(
        [
            lax.axis_index("blocks").astype(jnp.int32)[None],
            old_count,
            new_count,
            upwind[HALF : 2 * HALF].reshape(-1),
        ]
    )
    tab, up, dn = pl.pallas_call(
        functools.partial(faces_kernel, n, capacity),
        out_shape=(
            shape((T_SRC + 3 * capacity,), jnp.int32),
            shape((BINS, PACK), F32),
            shape((BINS, PACK), F32),
        ),
        in_specs=[smem, vmem, vmem],
        out_specs=(smem, vmem, vmem),
        compiler_params=params,
        name="faces",
    )(meta, spectra, courant)

    def along(value, step, ring):
        route = [(i, i + step) for i in range(n)]
        if ring:
            route = [(i, j % n) for i, j in route]
        return lax.ppermute(value, "blocks", [(i, j) for i, j in route if 0 <= j < n])

    from_prev, from_next = along(up, 1, True), along(dn, -1, True)
    weights = folded_kernel(kernel)

    def near(advance, value, name):
        return pl.pallas_call(
            functools.partial(near_kernel, capacity, advance),
            out_shape=blocks,
            in_specs=[smem, vmem, vmem],
            out_specs=vmem,
            compiler_params=params,
            cost_estimate=cost(10**7, 40 * 1024 * 1024),
            name=name,
        )(tab, value, courant)

    def first_local(b, where, q, cs, out):
        first_block(b, where, q, cs, out, None)

    def second_local(b, where, q, cs, out):
        second_block(b, where, q, cs, out, None, None)

    done = near(first_local, spectra, "first_near")
    packet = shape((BINS, 2 * PACK), F32)
    pool = pltpu.VMEM((2 * HALF + 4 * YZ, BINS, CELLS), F32)
    q1, up, dn = pl.pallas_call(
        functools.partial(first_kernel, capacity),
        out_shape=(blocks, packet, packet),
        in_specs=[smem, vmem, vmem, vmem, vmem, vmem],
        out_specs=(vmem, vmem, vmem),
        scratch_shapes=[pool],
        compiler_params=params,
        name="first",
    )(tab, spectra, courant, from_prev, from_next, done)
    from_prev, from_next = along(up, 1, True), along(dn, -1, True)
    done = near(second_local, q1, "second_near")
    done, weights = lax.optimization_barrier((done, weights))
    q2, up, dn = pl.pallas_call(
        functools.partial(second_kernel, capacity),
        out_shape=(blocks, half, half),
        in_specs=[smem, vmem, vmem, vmem, vmem, vmem],
        out_specs=(vmem, vmem, vmem),
        scratch_shapes=[pool, pool],
        compiler_params=params,
        name="second",
    )(tab, q1, courant, from_prev, from_next, done)
    from_prev, from_next = along(up, 1, False), along(dn, -1, False)
    buffers = [
        pltpu.VMEM((ROWS, CELLS), F32),
        pltpu.VMEM((ROWS, CELLS), F32),
        pltpu.VMEM((KDIM, CELLS), jnp.bfloat16),
        pltpu.VMEM((KDIM, CELLS), jnp.bfloat16),
        pltpu.VMEM((2, BINS, CELLS), F32),
    ]
    work = 2 * BINS * KDIM * CELLS
    updated = pl.pallas_call(
        functools.partial(stay_kernel, capacity),
        out_shape=blocks,
        in_specs=[smem, vmem, vmem],
        out_specs=hbm,
        scratch_shapes=buffers
        + [
            pltpu.VMEM((BINS, CELLS), F32),
            pltpu.SemaphoreType.DMA((2,)),
            pltpu.SemaphoreType.DMA,
        ],
        compiler_params=params,
        cost_estimate=cost(24 * work, 12 * 1024 * 1024),
        name="stay",
    )(tab, q2, weights)
    return pl.pallas_call(
        functools.partial(come_kernel, capacity),
        out_shape=blocks,
        in_specs=[smem, vmem, vmem, vmem, hbm],
        out_specs=hbm,
        input_output_aliases={4: 0},
        scratch_shapes=buffers + [pltpu.SemaphoreType.DMA((2,))],
        compiler_params=params,
        cost_estimate=cost(12 * work, 6 * 1024 * 1024),
        name="come",
    )(tab, from_prev, from_next, weights, updated)


def solution(mesh):
    in_specs = (P("blocks", None, None), P("blocks", None, None), P(), P(), P(), P())
    out_specs = P("blocks", None, None)
    return jax.shard_map(
        functools.partial(on_device, mesh.shape["blocks"]),
        mesh=mesh,
        in_specs=in_specs,
        out_specs=out_specs,
        check_vma=False,
    )
```

```python
import functools

import jax
import jax.numpy as jnp
from jax import lax
from jax.experimental import pallas as pl
from jax.experimental.pallas import tpu as pltpu
from jax.sharding import PartitionSpec as P

HALF = 12
BINS = 66
EDGE = 8
CELLS = 512
YZ = 6
PACK = HALF * 64 + 2 * CELLS
ROWS = 72
STRIDES = (64, 8, 1)
KDIM = 2816
VMEM_LIMIT = 63 * 1024 * 1024
CHUNKS = ((0, 16), (16, 32), (32, 48), (48, 64), (64, 66))
F32 = jnp.float32

T_OC, T_NC, T_OS, T_NS = 0, 1, 2, 3
T_SEND = 8
T_SRC = 32


def lane_coord(direction, rows):
    lane = lax.broadcasted_iota(jnp.int32, (rows, CELLS), 1)
    return (lane // STRIDES[direction]) % EDGE


def table_kernel(n, capacity, meta, tab):
    me = meta[0]

    def total(base, count):
        return lax.fori_loop(0, count, lambda i, s: s + meta[base + i], jnp.int32(0))

    old_start, new_start = total(1, me), total(1 + n, me)
    oc, nc = meta[1 + me], meta[1 + n + me]
    tab[T_OC] = oc
    tab[T_NC] = nc
    tab[T_OS] = old_start
    tab[T_NS] = new_start
    base = 1 + 2 * n
    end = old_start + oc
    zero = jnp.int32(0)
    end_run = lax.rem(end, HALF)
    start_run = lax.rem(old_start, HALF)

    def up(t, d):
        return meta[base + 3 * t + d] - HALF

    for d in (1, 2):
        for k in range(YZ):
            tab[T_SEND + (d - 1) * YZ + k] = zero
            tab[T_SEND + 2 * YZ + (d - 1) * YZ + k] = zero

    def block_src(b, carry):
        pos = lax.rem(old_start + b, HALF)
        rel = meta[base + 3 * pos] - HALF - pos
        u = b + rel
        tab[T_SRC + 3 * b] = jnp.where(
            u < 0, capacity + HALF + u, jnp.where(u >= oc, capacity + HALF + u - oc, u)
        )
        for d in (1, 2):
            tab[T_SRC + 3 * b + d] = jnp.clip(b + up(pos, d) - pos, 0, capacity - 1)
        return carry

    lax.fori_loop(0, capacity, block_src, zero)

    for d in (1, 2):
        pool = capacity + 2 * HALF + (d - 1) * 2 * YZ

        def link(t, counts):
            s_up, s_dn, r_up, r_dn = counts
            u = up(t, d)
            cross = (t >= end_run) & (u < end_run)

            @pl.when(cross)
            def _():
                tab[T_SEND + (d - 1) * YZ + s_up] = jnp.clip(oc - end_run + u, 0, capacity - 1)

            s_up = s_up + cross.astype(jnp.int32)
            cross = (t < end_run) & (u >= end_run)
            b = oc - end_run + t

            @pl.when(cross & (b >= 0))
            def _():
                tab[T_SRC + 3 * b + d] = pool + YZ + r_dn

            r_dn = r_dn + cross.astype(jnp.int32)
            cross = (t < start_run) & (u >= start_run)

            @pl.when(cross)
            def _():
                tab[T_SEND + 2 * YZ + (d - 1) * YZ + s_dn] = jnp.clip(
                    u - start_run, 0, capacity - 1
                )

            s_dn = s_dn + cross.astype(jnp.int32)
            cross = (t >= start_run) & (u < start_run)

            @pl.when(cross)
            def _():
                tab[T_SRC + 3 * jnp.minimum(t - start_run, capacity - 1) + d] = pool + r_up

            r_up = r_up + cross.astype(jnp.int32)
            return s_up, s_dn, r_up, r_dn

        lax.fori_loop(0, HALF, link, (zero, zero, zero, zero))


def pack(out, field, tab):
    oc = tab[T_OC]
    for r0, r1 in CHUNKS:
        low = lax.broadcasted_iota(jnp.int32, (r1 - r0, 128), 1) < 64
        coords = [lane_coord(d, r1 - r0) for d in (1, 2)]
        for side in range(2):
            first = oc - HALF if side == 0 else 0
            for j in range(0, HALF, 2):
                a = field(first + j, 0, r0, r1)[:, 384:]
                b = field(first + j + 1, 0, r0, r1)[:, 384:]
                out(side, r0, r1, 64 * j, jnp.where(low, pltpu.roll(a, 64, 1), b))
            for d in (1, 2):
                total = jnp.zeros((r1 - r0, CELLS), F32)
                for k in range(YZ):
                    block = tab[T_SEND + side * 2 * YZ + (d - 1) * YZ + k]
                    value = field(block, d, r0, r1)
                    shift = (CELLS - STRIDES[d] * (EDGE - 1 - k)) % CELLS
                    total = jnp.where(coords[d - 1] == k, pltpu.roll(value, shift, 1), total)
                out(side, r0, r1, HALF * 64 + (d - 1) * CELLS, total)


def unpack(packet, place, capacity):
    for r0, r1 in CHUNKS:
        for side in range(2):
            for j in range(HALF):
                value = packet(side, r0, r1, 128 * (j // 2), 128)
                if j % 2 == 0:
                    value = pltpu.roll(value, 64, 1)
                place(capacity + side * HALF + j, r0, r1, 384, value, 0)
            for d in (1, 2):
                value = packet(side, r0, r1, HALF * 64 + (d - 1) * CELLS, CELLS)
                for k in range(YZ):
                    slot = capacity + 2 * HALF + (d - 1) * 2 * YZ + side * YZ + k
                    place(slot, r0, r1, 0, pltpu.roll(value, STRIDES[d] * (EDGE - 1 - k), 1), d)


def shifted(value, upwind, direction, coord):
    if direction:
        upwind = pltpu.roll(upwind, CELLS - STRIDES[direction - 1], 1)
    return pltpu.roll(jnp.where(coord == EDGE - 1, upwind, value), STRIDES[direction], 1)


def faces_kernel(n, capacity, meta, q0, cs, tab, up, dn):
    table_kernel(n, capacity, meta, tab)
    outs = (up, dn)

    def field(block, d, r0, r1):
        return q0[block, r0:r1, :] * cs[block, d : d + 1, :]

    def out(side, r0, r1, lane, value):
        outs[side][r0:r1, lane : lane + value.shape[1]] = value

    pack(out, field, tab)


def first_kernel(capacity, tab, q0, cs, from_prev, from_next, q1, up, dn, pool):
    packets = (from_prev, from_next)

    def place(slot, r0, r1, l0, value, d):
        pool[slot - capacity, r0:r1, l0 : l0 + value.shape[1]] = value

    unpack(
        lambda side, r0, r1, lane, width: packets[side][r0:r1, lane : lane + width],
        place,
        capacity,
    )

    def step(b, carry):
        srcs = [tab[T_SRC + 3 * b + d] for d in range(3)]
        local = [jnp.minimum(s, capacity - 1) for s in srcs]
        far = [jnp.maximum(s - capacity, 0) for s in srcs]
        remote = [s >= capacity for s in srcs]
        for r0, r1 in CHUNKS:
            q = q0[b, r0:r1, :]
            result = q
            for d in range(3):
                coord = lane_coord(d, r1 - r0)
                flux = q * cs[b, d : d + 1, :]
                near = q0[local[d], r0:r1, :] * cs[local[d], d : d + 1, :]
                upwind = jnp.where(remote[d], pool[far[d], r0:r1, :], near)
                result = result - flux + shifted(flux, upwind, d, coord)
            q1[b, r0:r1, :] = result
        return carry

    lax.fori_loop(0, tab[T_OC], step, 0)

    outs = (up, dn)

    def flux_field(block, d, r0, r1):
        q = q1[block, r0:r1, :]
        c = cs[block, d : d + 1, :]
        m = q - pltpu.roll(q, STRIDES[d], 1)
        m = jnp.maximum(jnp.minimum(m, q), 0.0)
        return c * (q + (0.5 * (1.0 - c)) * m)

    def layer_field(block, d, r0, r1):
        return q1[block, r0:r1, :]

    for part, field in enumerate((flux_field, layer_field)):

        def out(side, r0, r1, lane, value, part=part):
            lane = lane + part * PACK
            outs[side][r0:r1, lane : lane + value.shape[1]] = value

        pack(out, field, tab)


def second_kernel(
    capacity, tab, q1, cs, from_prev, from_next, q2, mig_up, mig_dn, lpool, fx, fy, fz
):
    packets = (from_prev, from_next)
    fluxes = (fx, fy, fz)
    bases = (capacity, capacity + 2 * HALF, capacity + 2 * HALF + 2 * YZ)

    def place_layer(slot, r0, r1, l0, value, d):
        lpool[slot - capacity, r0:r1, l0 : l0 + value.shape[1]] = value

    def place_flux(slot, r0, r1, l0, value, d):
        fluxes[d][slot - bases[d] + capacity, r0:r1, l0 : l0 + value.shape[1]] = value

    for part, place in enumerate((place_flux, place_layer)):
        unpack(
            lambda side, r0, r1, lane, width, part=part: packets[side][
                r0:r1, part * PACK + lane : part * PACK + lane + width
            ],
            place,
            capacity,
        )

    def limit(b, carry):
        for d in range(3):
            src = tab[T_SRC + 3 * b + d]
            local = jnp.minimum(src, capacity - 1)
            far = jnp.maximum(src - capacity, 0)
            remote = src >= capacity
            c = cs[b, d : d + 1, :]
            half = 0.5 * (1.0 - c)
            for r0, r1 in CHUNKS:
                coord = lane_coord(d, r1 - r0)
                q = q1[b, r0:r1, :]
                upwind = jnp.where(remote, lpool[far, r0:r1, :], q1[local, r0:r1, :])
                m = q - shifted(q, upwind, d, coord)
                m = jnp.maximum(jnp.minimum(m, q), 0.0)
                fluxes[d][b, r0:r1, :] = c * (q + half * m)
        return carry

    lax.fori_loop(0, tab[T_OC], limit, 0)

    def step(b, carry):
        srcs = [tab[T_SRC + 3 * b + d] for d in range(3)]
        srcs = [
            jnp.where(srcs[d] >= capacity, srcs[d] - bases[d] + capacity, srcs[d])
            for d in range(3)
        ]
        for r0, r1 in CHUNKS:
            result = q1[b, r0:r1, :]
            for d in range(3):
                coord = lane_coord(d, r1 - r0)
                flux = fluxes[d][b, r0:r1, :]
                upwind = fluxes[d][srcs[d], r0:r1, :]
                result = result - flux + shifted(flux, upwind, d, coord)
            q2[b, r0:r1, :] = result
        return carry

    oc = tab[T_OC]
    lax.fori_loop(0, oc, step, 0)

    def copy(j, carry):
        mig_up[j] = q2[oc - HALF + j]
        mig_dn[j] = q2[j]
        return carry

    lax.fori_loop(0, HALF, copy, 0)


def build_pairs(q, qp, pairs):
    qp[0:BINS, :] = q
    qp[BINS : BINS + 1, :] = q[BINS - 1 : BINS, :]
    qp[BINS + 1 : BINS + 2, :] = q[BINS - 2 : BINS - 1, :]
    qp[BINS + 2 : ROWS, :] = jnp.zeros((ROWS - BINS - 2, CELLS), F32)
    row = lax.broadcasted_iota(jnp.int32, (8, CELLS), 0)
    pending = None
    at = 0
    for i in range(BINS - 2):
        lead = jnp.broadcast_to(qp[i : i + 1, :], (8, CELLS))
        for g in range(i // 8, ROWS // 8):
            by = lead
            if i < 2 and g == ROWS // 8 - 1:
                by = jnp.where(row < 2, lead, qp[BINS - 1 - i : BINS - i, :])
            term = by * qp[8 * g : 8 * g + 8, :]
            if pending is None:
                pending = term
            else:
                tile = jnp.concatenate([pending, term], axis=0)
                pairs[at : at + 16, :] = tile.astype(jnp.bfloat16)
                pending = None
                at += 16


def coalesce_range(lo, hi, load, w, out, qps, pairs, res, sems):
    def copy_out(slot, buf):
        return pltpu.make_async_copy(res.at[buf], out.at[slot], sems.at[buf])

    count = hi - lo

    def body(it, carry):
        first = lo + 2 * it
        slots = (first, jnp.minimum(first + 1, hi - 1))
        values = [load(s) for s in slots]

        @pl.when(it > 0)
        def _():
            for buf in range(2):
                copy_out(lo, buf).wait()

        for buf in range(2):
            build_pairs(values[buf], qps[buf], pairs[buf])
        for buf in range(2):
            gain = jnp.dot(w[...], pairs[buf][...], preferred_element_type=F32)
            res[buf] = qps[buf][0:BINS, :] + gain
        copy_out(slots[0], 0).start()

        @pl.when(first + 1 < hi)
        def _():
            copy_out(slots[1], 1).start()

        return carry

    trips = lax.div(count + 1, 2)
    lax.fori_loop(0, trips, body, 0)

    @pl.when(trips > 0)
    def _():
        copy_out(lo, 0).wait()

    @pl.when((trips > 0) & (lax.rem(count, 2) == 0))
    def _():
        copy_out(lo, 1).wait()


def stay_kernel(capacity, tab, q2, w, out, qpa, qpb, pa, pb, res, zero, sems, zsem):
    oc, nc, old, new = tab[T_OC], tab[T_NC], tab[T_OS], tab[T_NS]
    zero[...] = jnp.zeros_like(zero)

    def blank(slot):
        return pltpu.make_async_copy(zero, out.at[slot], zsem)

    def start(slot, carry):
        blank(slot).start()
        return carry

    def wait(slot, carry):
        blank(slot).wait()
        return carry

    lax.fori_loop(nc, capacity, start, 0)
    lo = jnp.clip(old - new, 0, nc)
    hi = jnp.clip(old + oc - new, lo, nc)
    coalesce_range(
        lo, hi, lambda s: q2[s + new - old], w, out, (qpa, qpb), (pa, pb), res, sems
    )
    lax.fori_loop(nc, capacity, wait, 0)


def come_kernel(capacity, tab, from_prev, from_next, w, old_out, out, qpa, qpb, pa, pb, res, sems):
    oc, nc, old, new = tab[T_OC], tab[T_NC], tab[T_OS], tab[T_NS]
    args = (w, out, (qpa, qpb), (pa, pb), res, sems)
    coalesce_range(
        jnp.int32(0),
        jnp.clip(old - new, 0, nc),
        lambda s: from_prev[s + new - old + HALF],
        *args,
    )
    coalesce_range(
        jnp.clip(old + oc - new, 0, nc),
        nc,
        lambda s: from_next[s + new - old - oc],
        *args,
    )


def folded_kernel(kernel):
    cube = kernel.reshape(BINS, BINS, BINS).astype(F32)
    turned = jnp.swapaxes(cube, 1, 2)
    i = lax.broadcasted_iota(jnp.int32, cube.shape, 1)
    j = lax.broadcasted_iota(jnp.int32, cube.shape, 2)
    folded = jnp.where(i < j, cube + turned, jnp.where(i == j, cube, 0.0))
    a, b = BINS - 2, BINS - 1
    extra = jnp.zeros((BINS, BINS, ROWS - BINS), F32)
    extra = extra.at[:, 0, 0].set(cube[:, b, b])
    extra = extra.at[:, 1, 0].set(cube[:, a, b] + cube[:, b, a])
    extra = extra.at[:, 1, 1].set(cube[:, a, a])
    wide = jnp.concatenate([folded, extra], axis=2).astype(jnp.bfloat16)
    parts = [
        wide[:, 8 * c : 8 * c + 8, 8 * c :].reshape(BINS, -1) for c in range(BINS // 8)
    ]
    return jnp.concatenate(parts, axis=1)


def on_device(n, spectra, courant, kernel, old_count, new_count, upwind):
    capacity = spectra.shape[0]
    shape = jax.ShapeDtypeStruct
    vmem = pl.BlockSpec(memory_space=pltpu.VMEM)
    smem = pl.BlockSpec(memory_space=pltpu.SMEM)
    hbm = pl.BlockSpec(memory_space=pl.ANY)
    params = pltpu.CompilerParams(vmem_limit_bytes=VMEM_LIMIT)
    blocks = shape((capacity, BINS, CELLS), F32)
    half = shape((HALF, BINS, CELLS), F32)

    def cost(flops, nbytes):
        return pl.CostEstimate(flops=flops, bytes_accessed=nbytes, transcendentals=0)

    meta = jnp.concatenate(
        [
            lax.axis_index("blocks").astype(jnp.int32)[None],
            old_count,
            new_count,
            upwind[HALF : 2 * HALF].reshape(-1),
        ]
    )
    tab, up, dn = pl.pallas_call(
        functools.partial(faces_kernel, n, capacity),
        out_shape=(
            shape((T_SRC + 3 * capacity,), jnp.int32),
            shape((BINS, PACK), F32),
            shape((BINS, PACK), F32),
        ),
        in_specs=[smem, vmem, vmem],
        out_specs=(smem, vmem, vmem),
        compiler_params=params,
        name="faces",
    )(meta, spectra, courant)

    def along(value, step, ring):
        route = [(i, i + step) for i in range(n)]
        if ring:
            route = [(i, j % n) for i, j in route]
        return lax.ppermute(value, "blocks", [(i, j) for i, j in route if 0 <= j < n])

    from_prev, from_next = along(up, 1, True), along(dn, -1, True)
    weights = folded_kernel(kernel)
    q1, up, dn = pl.pallas_call(
        functools.partial(first_kernel, capacity),
        out_shape=(blocks, shape((BINS, 2 * PACK), F32), shape((BINS, 2 * PACK), F32)),
        in_specs=[smem, vmem, vmem, vmem, vmem],
        out_specs=(vmem, vmem, vmem),
        scratch_shapes=[pltpu.VMEM((2 * HALF + 4 * YZ, BINS, CELLS), F32)],
        compiler_params=params,
        name="first",
    )(tab, spectra, courant, from_prev, from_next)
    from_prev, from_next = along(up, 1, True), along(dn, -1, True)
    q1, weights = lax.optimization_barrier((q1, weights))
    q2, up, dn = pl.pallas_call(
        functools.partial(second_kernel, capacity),
        out_shape=(blocks, half, half),
        in_specs=[smem, vmem, vmem, vmem, vmem],
        out_specs=(vmem, vmem, vmem),
        scratch_shapes=[
            pltpu.VMEM((2 * HALF + 4 * YZ, BINS, CELLS), F32),
            pltpu.VMEM((capacity + 2 * HALF, BINS, CELLS), F32),
            pltpu.VMEM((capacity + 2 * YZ, BINS, CELLS), F32),
            pltpu.VMEM((capacity + 2 * YZ, BINS, CELLS), F32),
        ],
        compiler_params=params,
        name="second",
    )(tab, q1, courant, from_prev, from_next)
    from_prev, from_next = along(up, 1, False), along(dn, -1, False)
    buffers = [
        pltpu.VMEM((ROWS, CELLS), F32),
        pltpu.VMEM((ROWS, CELLS), F32),
        pltpu.VMEM((KDIM, CELLS), jnp.bfloat16),
        pltpu.VMEM((KDIM, CELLS), jnp.bfloat16),
        pltpu.VMEM((2, BINS, CELLS), F32),
    ]
    work = 2 * BINS * KDIM * CELLS
    updated = pl.pallas_call(
        functools.partial(stay_kernel, capacity),
        out_shape=blocks,
        in_specs=[smem, vmem, vmem],
        out_specs=hbm,
        scratch_shapes=buffers
        + [
            pltpu.VMEM((BINS, CELLS), F32),
            pltpu.SemaphoreType.DMA((2,)),
            pltpu.SemaphoreType.DMA,
        ],
        compiler_params=params,
        cost_estimate=cost(24 * work, 12 * 1024 * 1024),
        name="stay",
    )(tab, q2, weights)
    return pl.pallas_call(
        functools.partial(come_kernel, capacity),
        out_shape=blocks,
        in_specs=[smem, vmem, vmem, vmem, hbm],
        out_specs=hbm,
        input_output_aliases={4: 0},
        scratch_shapes=buffers + [pltpu.SemaphoreType.DMA((2,))],
        compiler_params=params,
        cost_estimate=cost(12 * work, 6 * 1024 * 1024),
        name="come",
    )(tab, from_prev, from_next, weights, updated)


def solution(mesh):
    in_specs = (P("blocks", None, None), P("blocks", None, None), P(), P(), P(), P())
    out_specs = P("blocks", None, None)
    return jax.shard_map(
        functools.partial(on_device, mesh.shape["blocks"]),
        mesh=mesh,
        in_specs=in_specs,
        out_specs=out_specs,
        check_vma=False,
    )
```
